32 devices in a mesh: grp: 2 (over core), seq: 16 (over z, y, x).
Axes of the slice: x: 2, y: 2, z: 4, core: 2. Of those that a mesh axis runs over, the one named last changes fastest.
Arguments:
- prompt_x: bfloat16 [2, 2, 2048, 1024], P(None, 'grp', 'seq'), may hold values from -6 to 6
- cont_x: bfloat16 [2, 2, 64, 512, 1024], P(None, 'grp', 'seq'), may hold values from -6 to 6
- prompt_routes: int32 [2, 2, 2, 128], P(None, 'grp'), may hold values from 0 to 1023, as said below
- cont_routes: int32 [2, 2, 64, 64], P(None, 'grp', 'seq'), may hold values from 0 to 511, as said below
- cont_group: int32 [2, 2, 64], P(None, 'grp', 'seq'), may hold values from 0 to 1, as said below
- w_query: bfloat16 [1024, 1024], P(('grp', 'seq')), may hold values from -0.1875 to 0.1875
- w_key: bfloat16 [1024, 1024], P(('grp', 'seq')), may hold values from -0.1875 to 0.1875
- w_value: bfloat16 [1024, 1024], P(('grp', 'seq')), may hold values from -0.1875 to 0.1875
- w_out: bfloat16 [1024, 1024], P(('grp', 'seq')), may hold values from -1.5 to 1.5
- w_up: bfloat16 [1024, 4096], P(('grp', 'seq')), may hold values from -0.1875 to 0.1875
- w_down: bfloat16 [4096, 1024], P(('grp', 'seq')), may hold values from -0.09375 to 0.09375
- gain_attn: bfloat16 [1024], P(('grp', 'seq')), may hold values from 0.5 to 1.5
- gain_mlp: bfloat16 [1024], P(('grp', 'seq')), may hold values from 0.5 to 1.5
- w_router: bfloat16 [1024], P(('grp', 'seq')), may hold values from -0.1875 to 0.1875
- prompt_cot: bfloat16 [2, 2, 2048, 1024], P(None, 'grp', 'seq'), may hold values from -6 to 6
- cont_cot: bfloat16 [2, 2, 64, 512, 1024], P(None, 'grp', 'seq'), may hold values from -6 to 6
Outputs:
- prompt_out: bfloat16 [2, 2, 2048, 1024], P(None, 'grp', 'seq')
- cont_out: bfloat16 [2, 2, 64, 512, 1024], P(None, 'grp', 'seq')
- prompt_grad: bfloat16 [2, 2, 2048, 1024], P(None, 'grp', 'seq')
- cont_grad: bfloat16 [2, 2, 64, 512, 1024], P(None, 'grp', 'seq')
- grad_query: float32 [1024, 1024], P(('grp', 'seq'))
- grad_key: float32 [1024, 1024], P(('grp', 'seq'))
- grad_value: float32 [1024, 1024], P(('grp', 'seq'))
- grad_out: float32 [1024, 1024], P(('grp', 'seq'))
- grad_up: float32 [1024, 4096], P(('grp', 'seq'))
- grad_down: float32 [4096, 1024], P(('grp', 'seq'))
- grad_gain_attn: float32 [1024], P(('grp', 'seq'))
- grad_gain_mlp: float32 [1024], P(('grp', 'seq'))
- grad_router: float32 [1024], P(('grp', 'seq'))
The draws below stay inside these ranges and needn't reach their ends.
Inputs may be any that keep to these rules, and one draw needn't show every extreme that they name: `prompt_routes`: each row lists 128 distinct positions of one prompt in increasing order, always including the first and the last; the 128 positions k * 128 to (k + 1) * 128 - 1 hold at most 24 of them for every k, and exactly 24 for some k in every row. `cont_routes`: each row lists 64 distinct positions of one continuation in increasing order, always including the first and the last. `cont_group`: in each micro-batch and grp index, half of the 64 continuations name prompt 0 and half name prompt 1.
All inputs are finite; a program needn't handle non-finite values.
Results may differ from the reference program's by a relative error of at most 0.017.
Values may be sent and summed in bfloat16 or wider, within the bound.
A program may use at most 320 MiB of HBM per device.

```python
import jax
import jax.numpy as jnp
from jax import lax

D = 1024
HD = 64
FF = 4096
P_DEV = 128
PROMPT = 1024
KP = 128
L = 512
KC = 64
CONTS = 64
MB = 2
N_GRP = 2
N_SEQ = 16


def prompt_route_one(key_one):
    slices = PROMPT // P_DEV
    mean_count = P_DEV // 8
    key_list = jax.random.split(key_one, 3)
    slice_order = jax.random.permutation(key_list[0], slices)
    shifted = jax.random.randint(key_list[1], (slices // 2,), 0, mean_count // 2 + 1)
    shifted = shifted.at[0].set(mean_count // 2)
    counts = jnp.zeros((slices,), jnp.int32)
    counts = counts.at[slice_order[0::2]].set(mean_count + shifted)
    counts = counts.at[slice_order[1::2]].set(mean_count - shifted)
    scores = jax.random.randint(key_list[2], (slices, P_DEV), 0, 2 ** 20) * P_DEV + jnp.arange(P_DEV, dtype=jnp.int32)[None, :]
    scores = scores.at[0, 0].set(-2)
    scores = scores.at[slices - 1, P_DEV - 1].set(-1)
    rank_of = jnp.argsort(jnp.argsort(scores, axis=1), axis=1)
    chosen = (rank_of < counts[:, None]).reshape(-1)
    return jnp.nonzero(chosen, size=KP)[0].astype(jnp.int32)


def draw_prompt_routes(key, part):
    total_rows = MB * N_GRP * 2
    key_list = jax.random.split(jax.random.fold_in(key, 11), total_rows)
    return jax.vmap(prompt_route_one)(key_list).reshape(MB, N_GRP, 2, KP)


def cont_route_one(key_one):
    scores = jax.random.randint(key_one, (L,), 0, 2 ** 20) * L + jnp.arange(L, dtype=jnp.int32)
    scores = scores.at[0].set(-2)
    scores = scores.at[L - 1].set(-1)
    rank_of = jnp.argsort(jnp.argsort(scores))
    return jnp.nonzero(rank_of < KC, size=KC)[0].astype(jnp.int32)


def draw_cont_routes(key, part):
    total_rows = MB * N_GRP * CONTS
    key_list = jax.random.split(jax.random.fold_in(key, 23), total_rows)
    return jax.vmap(cont_route_one)(key_list).reshape(MB, N_GRP, CONTS, KC)


def group_one(key_one):
    shuffled = jax.random.permutation(key_one, CONTS)
    return (shuffled >= CONTS // 2).astype(jnp.int32)


def draw_cont_group(key, part):
    total_rows = MB * N_GRP
    key_list = jax.random.split(jax.random.fold_in(key, 37), total_rows)
    return jax.vmap(group_one)(key_list).reshape(MB, N_GRP, CONTS)


def block_scale(own_key, dims, cuts, smallest, high):
    def one(dim, parts):
        draws = jax.random.uniform(jax.random.fold_in(jax.random.fold_in(own_key, 6), dim), (parts,), jnp.float32, smallest / len(cuts), high / len(cuts))
        return jnp.repeat(jnp.exp(draws), dims[dim] // parts).reshape((-1,) + (1,) * (len(dims) - dim - 1))

    level = one(*cuts[0])
    for cut in cuts[1:]:
        level = level * one(*cut)
    return level


def scatter_about(stream_key, extent, deviation, most, pieces=(), held_as=jnp.bfloat16):
    array = deviation * jax.random.normal(stream_key, extent, jnp.float32)
    if pieces:
        array = array * block_scale(stream_key, extent, pieces, -0.22, 0.18)
    return jnp.clip(array, -most, most).astype(held_as)


def setup_inputs(seed: int = 0) -> dict:
    seeds = jax.random.split(jax.random.key(seed), 17)
    return {
        "prompt_x": scatter_about(seeds[0], (MB, N_GRP, N_SEQ * P_DEV, D), 1.0, 6.0, ((1, 2), (2, 16))),
        "cont_x": scatter_about(seeds[1], (MB, N_GRP, CONTS, L, D), 1.0, 6.0, ((1, 2), (2, 16))),
        "prompt_routes": draw_prompt_routes(jax.random.fold_in(seeds[16], 71), 0),
        "cont_routes": draw_cont_routes(jax.random.fold_in(seeds[16], 71), 0),
        "cont_group": draw_cont_group(jax.random.fold_in(seeds[16], 71), 0),
        "w_query": scatter_about(seeds[5], (D, D), D ** -0.5, 0.1875, ((0, 32),)),
        "w_key": scatter_about(seeds[6], (D, D), D ** -0.5, 0.1875, ((0, 32),)),
        "w_value": scatter_about(seeds[7], (D, D), D ** -0.5, 0.1875, ((0, 32),)),
        "w_out": scatter_about(seeds[8], (D, D), (D // 64) ** -0.5, 1.5, ((0, 32),)),
        "w_up": scatter_about(seeds[9], (D, FF), D ** -0.5, 0.1875, ((0, 32),)),
        "w_down": scatter_about(seeds[10], (FF, D), FF ** -0.5, 0.09375, ((0, 32),)),
        "gain_attn": jnp.clip(1.0 + 0.1 * jax.random.normal(seeds[11], (D,), jnp.float32), 0.5, 1.5).astype(jnp.bfloat16),
        "gain_mlp": jnp.clip(1.0 + 0.1 * jax.random.normal(seeds[12], (D,), jnp.float32), 0.5, 1.5).astype(jnp.bfloat16),
        "w_router": scatter_about(seeds[13], (D,), D ** -0.5, 0.1875, ((0, 32),)),
        "prompt_cot": scatter_about(seeds[14], (MB, N_GRP, N_SEQ * P_DEV, D), 1.0, 6.0, ((1, 2), (2, 16))),
        "cont_cot": scatter_about(seeds[15], (MB, N_GRP, CONTS, L, D), 1.0, 6.0, ((1, 2), (2, 16))),
    }


EPS = 1e-05
SCALE = 0.125
NEGATIVE = -1e+30
ROOT = 0.7978845608028654

@jax.custom_vjp
def low(v):
    return lax.optimization_barrier(v.astype(jnp.bfloat16)).astype(jnp.float32)

@jax.custom_vjp
def low_back(v):
    return v

def low_keep(v):
    return (low(v), None)

def low_pass(kept, grad):
    return (grad,)

def back_keep(v):
    return (v, None)

def back_low(kept, grad):
    return (low(grad),)
low.defvjp(low_keep, low_pass)
low_back.defvjp(back_keep, back_low)

def matmul(left, right):
    return jnp.dot(left, right, precision=lax.Precision.HIGHEST)

def normed(values, gain_vec):
    return values * lax.rsqrt(lax.optimization_barrier(jnp.mean(values * values, -1, keepdims=True)) + EPS) * gain_vec

def gelu_tanh(values):
    return 0.5 * values * (1.0 + jnp.tanh(ROOT * (values + 0.044715 * values * values * values)))

def project(token_rows, weight_mat):
    return low_back(low(matmul(token_rows, weight_mat)))

def attend(query_heads, key_heads, value_heads, key_mask):
    raw_scores = jnp.einsum('qhd,khd->hqk', query_heads, key_heads, precision=lax.Precision.HIGHEST)
    scores = low_back(raw_scores * SCALE)
    masked = jnp.where(key_mask[None], scores, NEGATIVE)
    row_max = lax.optimization_barrier(jnp.max(masked, -1, keepdims=True))
    exp_scores = jnp.exp(masked - row_max)
    attn_probs = low(exp_scores / lax.optimization_barrier(jnp.sum(exp_scores, -1, keepdims=True)))
    return jnp.einsum('hqk,khd->qhd', attn_probs, value_heads, precision=lax.Precision.HIGHEST)

def one_row(params, prompt_rows, cont_rows, prompt_index, cont_index, cont_prompt):
    query_mat, key_mat, value_mat, out_mat, up_mat, down_mat, attn_gain, mlp_gain, router_vec = params
    width = prompt_rows.shape[1]
    prompt_len = prompt_rows.shape[0] // 2
    routed_prompt = prompt_index.shape[1]
    conts, routed = cont_index.shape
    heads = width // HD
    flat_index = (prompt_index + jnp.arange(2, dtype=jnp.int32)[:, None] * prompt_len).reshape(-1)
    picked_prompt = prompt_rows[flat_index]
    picked_cont = jnp.take_along_axis(cont_rows, cont_index[:, :, None], 1).reshape(conts * routed, width)
    token_rows = jnp.concatenate([picked_prompt, picked_cont], 0)
    first = low(normed(token_rows, attn_gain))
    queries = project(first, query_mat).reshape(-1, heads, HD)
    keys_all = project(first, key_mat).reshape(-1, heads, HD)
    values_all = project(first, value_mat).reshape(-1, heads, HD)
    prompt_rows_n = 2 * routed_prompt
    causal_prompt = jnp.tril(jnp.ones((routed_prompt, routed_prompt), dtype=bool))
    prompt_q = queries[:prompt_rows_n].reshape(2, routed_prompt, heads, HD)
    prompt_k = keys_all[:prompt_rows_n].reshape(2, routed_prompt, heads, HD)
    prompt_v = values_all[:prompt_rows_n].reshape(2, routed_prompt, heads, HD)
    prompt_att = jax.vmap(lambda qh, kh, vh: attend(qh, kh, vh, causal_prompt))(prompt_q, prompt_k, prompt_v)
    cont_mask = jnp.concatenate([jnp.ones((routed, routed_prompt), dtype=bool), jnp.tril(jnp.ones((routed, routed), dtype=bool))], 1)
    cont_q = queries[prompt_rows_n:].reshape(conts, routed, heads, HD)
    cont_k = jnp.concatenate([prompt_k[cont_prompt], keys_all[prompt_rows_n:].reshape(conts, routed, heads, HD)], 1)
    cont_v = jnp.concatenate([prompt_v[cont_prompt], values_all[prompt_rows_n:].reshape(conts, routed, heads, HD)], 1)
    cont_att = jax.vmap(lambda qh, kh, vh: attend(qh, kh, vh, cont_mask))(cont_q, cont_k, cont_v)
    attended = low_back(low(jnp.concatenate([prompt_att.reshape(prompt_rows_n, width), cont_att.reshape(conts * routed, width)], 0)))
    branch_a = low_back(matmul(attended, out_mat))
    hidden = token_rows + branch_a
    second = low(normed(hidden, mlp_gain))
    up_proj = low_back(matmul(second, up_mat))
    gelu_out = low(gelu_tanh(up_proj))
    branch_m = low_back(matmul(gelu_out, down_mat))
    router_logit = matmul(token_rows, router_vec)
    router_score = 1.0 / (1.0 + jnp.exp(-router_logit))
    result = token_rows + router_score[:, None] * (branch_a + branch_m)
    new_prompt = prompt_rows.at[flat_index].set(result[:prompt_rows_n])
    new_cont = cont_rows.at[jnp.arange(conts, dtype=jnp.int32)[:, None], cont_index].set(result[prompt_rows_n:].reshape(conts, routed, width))
    return (new_prompt, new_cont)

def reference(prompt_x, cont_x, prompt_routes, cont_routes, cont_group, w_query, w_key, w_value, w_out, w_up, w_down, gain_attn, gain_mlp, w_router, prompt_cot, cont_cot):
    float_args = (w_query, w_key, w_value, w_out, w_up, w_down, gain_attn, gain_mlp, w_router)
    params = tuple((weight_arr.astype(jnp.float32) for weight_arr in float_args))
    row_count = prompt_x.shape[0] * prompt_x.shape[1]
    prompt_flat = prompt_x.astype(jnp.float32).reshape((row_count,) + prompt_x.shape[2:])
    cont_flat = cont_x.astype(jnp.float32).reshape((row_count,) + cont_x.shape[2:])
    route_items = (prompt_routes.reshape((row_count,) + prompt_routes.shape[2:]), cont_routes.reshape((row_count,) + cont_routes.shape[2:]), cont_group.reshape((row_count,) + cont_group.shape[2:]))

    def forward(param_set, prompt_all, cont_all):
        step_fn = jax.checkpoint(lambda row_items: one_row(param_set, *row_items))
        return lax.map(step_fn, (prompt_all, cont_all) + route_items)
    outputs, backward = jax.vjp(forward, params, prompt_flat, cont_flat)
    prompt_cot_flat = prompt_cot.astype(jnp.float32).reshape(prompt_flat.shape)
    cont_cot_flat = cont_cot.astype(jnp.float32).reshape(cont_flat.shape)
    param_grads, prompt_grads, cont_grads = backward((prompt_cot_flat, cont_cot_flat))
    return (outputs[0].reshape(prompt_x.shape).astype(jnp.bfloat16), outputs[1].reshape(cont_x.shape).astype(jnp.bfloat16), prompt_grads.reshape(prompt_x.shape).astype(jnp.bfloat16), cont_grads.reshape(cont_x.shape).astype(jnp.bfloat16), param_grads[0], param_grads[1], param_grads[2], param_grads[3], param_grads[4], param_grads[5], param_grads[6], param_grads[7], param_grads[8])
```

```python
import functools

import jax
import jax.numpy as jnp
from jax import lax
from jax.experimental import pallas as pl
from jax.experimental.pallas import tpu as pltpu
from jax.sharding import PartitionSpec as P

HD = 64
EPS = 1e-05
SCALE = 0.125
NEGATIVE = -1e30
ROOT = 0.7978845608028654
FAR = 1 << 20
PPAD = 32
MESH = pl.DeviceIdType.MESH
ANY = pl.BlockSpec(memory_space=pl.ANY)
BF = jnp.bfloat16
F32 = jnp.float32
ZYX = (4, 2, 2)


def coords():
    g = lax.axis_index("grp")
    s = lax.axis_index("seq")
    return g, s, s // 4, (s // 2) % 2, s % 2


def partners():
    g, s, z, y, x = coords()
    out = {
        "x": (g, z * 4 + y * 2 + (1 - x)),
        "y": (g, z * 4 + (1 - y) * 2 + x),
        "s": (1 - g, s),
    }
    for k in (1, 2, 3):
        out["z%d" % k] = (g, ((z + k) % 4) * 4 + y * 2 + x)
    return out


def entry_barrier(where):
    sem = pltpu.get_barrier_semaphore()
    names = ("x", "y", "s", "z1", "z2", "z3")
    for name in names:
        pl.semaphore_signal(sem, inc=1, device_id=where[name], device_id_type=MESH)
    pl.semaphore_wait(sem, len(names))


def gather_kernel(routes, look, *refs):
    n = len(routes)
    ins, outs = refs[:n], refs[n : 2 * n]
    send_sem, recv_sem, local_sem = refs[2 * n :]
    g, s, z, y, x = coords()
    where = partners()
    entry_barrier(where)
    both = [r.isupper() for r in routes]
    zs = [z, (z + 1) % 4, (z + 3) % 4, (z + 2) % 4]

    def place(k, dy, dx):
        return (g, zs[k] * 4 + (1 - y if dy else y) * 2 + (1 - x if dx else x))

    def slot(p, who):
        return outs[p].at[who[0], who[1]] if both[p] else outs[p].at[who[1]]

    sends = []
    copies = []

    def send(p, who, to, own=False):
        src = ins[p] if own else slot(p, who)
        copy = pltpu.make_async_remote_copy(
            src,
            slot(p, who),
            send_sem.at[len(sends)],
            recv_sem.at[who[0], who[1], p],
            device_id=where[to],
            device_id_type=MESH,
        )
        copy.start()
        sends.append(copy)

    def wait(p, who):
        ref = slot(p, who)
        pltpu.make_async_remote_copy(
            ref,
            ref,
            send_sem.at[0],
            recv_sem.at[who[0], who[1], p],
            device_id=where["x"],
            device_id_type=MESH,
        ).wait_recv()

    def across(p, who):
        if both[p]:
            send(p, who, "s")

    def own(p):
        copy = pltpu.make_async_copy(ins[p], slot(p, (g, s)), local_sem.at[p])
        copy.start()
        copies.append(copy)
        for to in ("z1", "z3", "z2", "x", "y"):
            send(p, (g, s), to, True)
        if both[p]:
            send(p, (g, s), "s", True)

    def from_z(p):
        for k in (1, 2, 3):
            who = place(k, 0, 0)
            wait(p, who)
            send(p, who, "x")
            send(p, who, "y")
            across(p, who)

    def from_xy(p):
        for k in range(4):
            who = place(k, 0, 1)
            wait(p, who)
            if routes[p] in "Aa":
                send(p, who, "y")
            across(p, who)
            who = place(k, 1, 0)
            wait(p, who)
            if routes[p] in "Bb":
                send(p, who, "x")
            across(p, who)

    def diagonal(p):
        for k in range(4):
            who = place(k, 1, 1)
            wait(p, who)
            across(p, who)

    def from_core(p):
        if both[p]:
            for k in range(4):
                for dy in (0, 1):
                    for dx in (0, 1):
                        wait(p, (1 - g, place(k, dy, dx)[1]))

    for p in range(min(look, n)):
        own(p)
    for t in range(n + 3):
        if t + look < n:
            own(t + look)
        if t < n:
            from_z(t)
        if 0 <= t - 1 < n:
            from_xy(t - 1)
        if 0 <= t - 2 < n:
            diagonal(t - 2)
        if 0 <= t - 3 < n:
            from_core(t - 3)
    for copy in copies:
        copy.wait()
    for copy in sends:
        copy.wait_send()


def gather_call(arrays, routes, look):
    n = len(arrays)
    count = sum(31 if r.isupper() else 15 for r in routes)
    shapes = [
        jax.ShapeDtypeStruct(((2, 16) if r.isupper() else (16,)) + a.shape, a.dtype)
        for a, r in zip(arrays, routes)
    ]
    return pl.pallas_call(
        functools.partial(gather_kernel, routes, look),
        out_shape=shapes,
        in_specs=[ANY] * n,
        out_specs=[ANY] * n,
        scratch_shapes=[
            pltpu.SemaphoreType.DMA((count,)),
            pltpu.SemaphoreType.DMA((2, 16, n)),
            pltpu.SemaphoreType.DMA((n,)),
        ],
        compiler_params=pltpu.CompilerParams(collective_id=1, has_side_effects=True),
        name="gather_weights",
    )(*arrays)


def make_pieces(prompt_parts, rows):
    pieces = []

    def add(src, r0, count, c0, cols, both=True, dtype=BF):
        pieces.append(
            dict(src=src, r0=r0, rows=count, c0=c0, cols=cols, both=both, dtype=dtype)
        )

    for r in range(0, 128, rows):
        add(5, r, rows, 0, 1024)
    for c in range(4):
        for r in range(0, 32, rows):
            add(4, r, rows, c * 1024, 1024)
    for i in (3, 0, 1, 2):
        for r in range(0, 32, rows):
            add(i, r, rows, 0, 1024)
    add(6, 0, 8, 0, 128, True, F32)
    for j in range(prompt_parts):
        add(7 + j, 0, 24, 0, 1024, False)
    scratch = []
    for i, piece in enumerate(pieces):
        piece["order"] = (2, 1, 0) if i % 2 == 0 else (1, 2, 0)
        piece["bufs"] = {}
        tail = (piece["rows"], piece["cols"])

        def buf(name, shape):
            piece["bufs"][name] = len(scratch)
            scratch.append(pltpu.VMEM(shape + tail, piece["dtype"]))

        dims = list(ZYX)
        buf("own", tuple(dims))
        if piece["both"]:
            buf("other", tuple(dims))
        for stage, axis in enumerate(piece["order"]):
            size = dims[axis]
            dims[axis] = 1
            buf("recv%d" % stage, (size - 1,) + tuple(dims))
            if stage < 2:
                buf("sum%d" % stage, tuple(dims))
    return pieces, scratch


def one_along(ref, axis, start):
    index = [slice(None)] * 3
    index[axis] = pl.ds(start, 1)
    return ref.at[tuple(index)]


def scatter_kernel(pieces, n_in, n_out, n_buf, *refs):
    ins, outs = refs[:n_in], refs[n_in : n_in + n_out]
    bufs = refs[n_in + n_out : n_in + n_out + n_buf]
    send_sem, recv_sem, local_sem = refs[n_in + n_out + n_buf :]
    g, s, z, y, x = coords()
    me = (z, y, x)
    where = partners()
    entry_barrier(where)
    pending = []
    n_local = [0]

    def buf(piece, name):
        return bufs[piece["bufs"][name]]

    def push(src, dst, to):
        i = len(pending)
        copy = pltpu.make_async_remote_copy(
            src,
            dst,
            send_sem.at[i],
            recv_sem.at[i],
            device_id=where[to],
            device_id_type=MESH,
        )
        copy.start()
        pending.append(copy)
        return copy

    def window(piece, half):
        ref = ins[piece["src"]]
        index = (slice(None),) * 3 + (
            pl.ds(piece["r0"], piece["rows"]),
            pl.ds(piece["c0"], piece["cols"]),
        )
        return ref.at[(half,) + index] if piece["both"] else ref.at[index]

    def begin(piece):
        if piece["both"]:
            piece["across"] = push(window(piece, 1 - g), buf(piece, "other"), "s")
        copy = pltpu.make_async_copy(
            window(piece, g), buf(piece, "own"), local_sem.at[n_local[0]]
        )
        n_local[0] += 1
        copy.start()
        piece["load"] = copy

    def add_up(reads, dims, write):
        count = dims[0] * dims[1] * dims[2]

        def body(i, carry):
            iz = i // (dims[1] * dims[2])
            rest = i % (dims[1] * dims[2])
            at = (iz, rest // dims[2], rest % dims[2])
            total = None
            for read in reads:
                value = read(*at).astype(F32)
                total = value if total is None else total + value
            write(at, total)
            return carry

        if count == 1:
            body(0, 0)
        else:
            lax.fori_loop(0, count, body, 0)

    def exchange(piece, stage, cur):
        axis = piece["order"][stage]
        recv = buf(piece, "recv%d" % stage)
        if axis == 2:
            got = [push(one_along(cur, 2, 1 - x), recv.at[0], "x")]
        elif axis == 1:
            got = [push(one_along(cur, 1, 1 - y), recv.at[0], "y")]
        else:
            got = [
                push(one_along(cur, 0, (z + k) % 4), recv.at[k - 1], "z%d" % k)
                for k in (1, 3, 2)
            ]
        piece["got%d" % stage] = got

    def first(piece):
        piece["load"].wait()
        own = buf(piece, "own")
        if piece["both"]:
            piece["across"].wait_recv()
            other = buf(piece, "other")

            def write(at, total):
                own[at] = total.astype(own.dtype)

            add_up([lambda *at: own[at], lambda *at: other[at]], ZYX, write)
        piece["dims"] = list(ZYX)
        piece["cur"] = own
        exchange(piece, 0, own)

    def reduce(piece, stage):
        axis = piece["order"][stage]
        for copy in piece["got%d" % stage]:
            copy.wait_recv()
        cur = piece["cur"]
        recv = buf(piece, "recv%d" % stage)
        size = piece["dims"][axis]
        piece["dims"][axis] = 1

        def mine(*at):
            at = list(at)
            at[axis] = me[axis]
            return cur[tuple(at)]

        reads = [mine]
        for j in range(size - 1):
            reads.append(lambda *at, j=j: recv[(j,) + at])
        if stage < 2:
            dst = buf(piece, "sum%d" % stage)

            def write(at, total):
                dst[at] = total.astype(dst.dtype)

            add_up(reads, piece["dims"], write)
            piece["cur"] = dst
            exchange(piece, stage + 1, dst)
        else:
            out = outs[piece["src"]]

            def write(at, total):
                out[
                    pl.ds(piece["r0"], piece["rows"]), pl.ds(piece["c0"], piece["cols"])
                ] = total

            add_up(reads, piece["dims"], write)

    n = len(pieces)
    for piece in pieces:
        begin(piece)
    for t in range(n + 3):
        if t < n:
            first(pieces[t])
        for stage in range(3):
            if 0 <= t - 1 - stage < n:
                reduce(pieces[t - 1 - stage], stage)
    for copy in pending:
        copy.wait_send()


def scatter_call(arrays, out_shapes, prompt_parts, rows):
    pieces, scratch = make_pieces(prompt_parts, rows)
    remote = sum(6 if piece["both"] else 5 for piece in pieces)
    vmem = pl.BlockSpec(memory_space=pltpu.VMEM)
    return pl.pallas_call(
        functools.partial(
            scatter_kernel, pieces, len(arrays), len(out_shapes), len(scratch)
        ),
        out_shape=[jax.ShapeDtypeStruct(shape, F32) for shape in out_shapes],
        in_specs=[ANY] * len(arrays),
        out_specs=[vmem] * len(out_shapes),
        scratch_shapes=scratch
        + [
            pltpu.SemaphoreType.DMA((remote,)),
            pltpu.SemaphoreType.DMA((remote,)),
            pltpu.SemaphoreType.DMA((len(pieces),)),
        ],
        compiler_params=pltpu.CompilerParams(
            collective_id=2, has_side_effects=True, vmem_limit_bytes=60 << 20
        ),
        name="reduce_grads",
    )(*arrays)


def place_rows_kernel(idx_ref, new_ref, old_ref, out_ref):
    length, count = old_ref.shape[1], new_ref.shape[1]
    spot = lax.broadcasted_iota(jnp.int32, (length, count), 0)
    hit = spot == idx_ref[0]
    pick = jnp.where(hit, 1.0, 0.0)
    routed = jnp.sum(pick, axis=1, keepdims=True) > 0.5
    moved = jnp.dot(pick.astype(BF), new_ref[0], preferred_element_type=F32)
    out_ref[0] = jnp.where(routed, moved.astype(BF), old_ref[0])


def place_rows(old, idx, new):
    blocks, length, width = old.shape
    count = idx.shape[1]
    return pl.pallas_call(
        place_rows_kernel,
        out_shape=jax.ShapeDtypeStruct(old.shape, old.dtype),
        grid=(blocks,),
        in_specs=[
            pl.BlockSpec((1, 1, count), lambda b: (b, 0, 0)),
            pl.BlockSpec((1, count, width), lambda b: (b, 0, 0)),
            pl.BlockSpec((1, length, width), lambda b: (b, 0, 0)),
        ],
        out_specs=pl.BlockSpec((1, length, width), lambda b: (b, 0, 0)),
        name="place_rows",
    )(idx[:, None, :], new, old)


def stacked(pair):
    left = lax.broadcasted_iota(jnp.int32, pair.shape, 1) < HD
    zero = jnp.zeros_like(pair)
    return jnp.concatenate([jnp.where(left, pair, zero), jnp.where(left, zero, pair)], 0)


def unstacked(both):
    rows = both.shape[0] // 2
    left = lax.broadcasted_iota(jnp.int32, (rows, both.shape[1]), 1) < HD
    return jnp.where(left, both[:rows], both[rows:])


def dot_nt(a, b):
    return lax.dot_general(a, b, (((1,), (1,)), ((), ())), preferred_element_type=F32)


def dot_tn(a, b):
    return lax.dot_general(a, b, (((0,), (0,)), ((), ())), preferred_element_type=F32)


def probabilities(q2, keys, seen):
    scores = dot_nt(q2, keys) * SCALE
    masked = jnp.where(seen, scores, NEGATIVE)
    raised = jnp.exp(masked - jnp.max(masked, -1, keepdims=True))
    return raised / jnp.sum(raised, -1, keepdims=True)


def seen_cont(meta_row, rows, slots):
    own = (
        lax.broadcasted_iota(jnp.int32, (2 * rows, rows), 1)
        <= lax.broadcasted_iota(jnp.int32, (2 * rows, rows), 0) % rows
    )
    ours = jnp.broadcast_to(meta_row < FAR, (2 * rows, slots))
    return jnp.concatenate([ours.astype(jnp.int32), own.astype(jnp.int32)], 1) > 0


def seen_prompt(meta_row, rank_col):
    return meta_row <= jnp.concatenate([rank_col, rank_col], 0)


def attend_cont_kernel(sel, q_ref, k_ref, v_ref, kp_ref, vp_ref, meta_ref, o_ref):
    rows, slots = q_ref.shape[0], kp_ref.shape[1]
    seen = seen_cont(meta_ref[0], rows, slots)
    for pair in range(q_ref.shape[1] // 128):
        lanes = pl.ds(pair * 128, 128)
        keys = jnp.concatenate([kp_ref[0, :, lanes], k_ref[:, lanes]], 0)
        values = jnp.concatenate([vp_ref[0, :, lanes], v_ref[:, lanes]], 0)
        probs = probabilities(stacked(q_ref[:, lanes]), keys, seen)
        out = jnp.dot(probs.astype(BF), values, preferred_element_type=F32)
        o_ref[:, lanes] = unstacked(out).astype(BF)


def attend_prompt_kernel(sel, q_ref, rank_ref, kp_ref, vp_ref, meta_ref, o_ref):
    seen = seen_prompt(meta_ref[0], rank_ref[0])
    for pair in range(q_ref.shape[1] // 128):
        lanes = pl.ds(pair * 128, 128)
        probs = probabilities(stacked(q_ref[:, lanes]), kp_ref[0, :, lanes], seen)
        out = jnp.dot(probs.astype(BF), vp_ref[0, :, lanes], preferred_element_type=F32)
        o_ref[:, lanes] = unstacked(out).astype(BF)


def score_grads(probs, do2, values):
    grads = dot_nt(do2, values)
    inner = jnp.sum(probs * grads, -1, keepdims=True)
    return (probs * (grads - inner)).astype(BF)


def back_prompt_kernel(
    sel, q_ref, do_ref, rank_ref, kp_ref, vp_ref, meta_ref, dq_ref, dk_ref, dv_ref
):
    seen = seen_prompt(meta_ref[0], rank_ref[0])
    for pair in range(q_ref.shape[1] // 128):
        lanes = pl.ds(pair * 128, 128)
        q2, do2 = stacked(q_ref[:, lanes]), stacked(do_ref[:, lanes])
        keys, values = kp_ref[0, :, lanes], vp_ref[0, :, lanes]
        probs = probabilities(q2, keys, seen)
        ds = score_grads(probs, do2, values)
        dq = jnp.dot(ds, keys, preferred_element_type=F32)
        dq_ref[:, lanes] = (unstacked(dq) * SCALE).astype(BF)
        dk_ref[0, :, lanes] = dot_tn(ds, q2) * SCALE
        dv_ref[0, :, lanes] = dot_tn(probs.astype(BF), do2)


def back_cont_kernel(
    sel,
    sel_prompt,
    q_ref,
    k_ref,
    v_ref,
    do_ref,
    kp_ref,
    vp_ref,
    meta_ref,
    dk_first,
    dv_first,
    dq_ref,
    dk_ref,
    dv_ref,
    dkp_ref,
    dvp_ref,
):
    rows, slots = q_ref.shape[0], kp_ref.shape[1]
    step = pl.program_id(0)

    @pl.when(step == 0)
    def _():
        dkp_ref[...] = jnp.zeros_like(dkp_ref)
        dvp_ref[...] = jnp.zeros_like(dvp_ref)
        for m in range(dk_first.shape[0]):
            dkp_ref[sel_prompt[m]] = dk_first[m]
            dvp_ref[sel_prompt[m]] = dv_first[m]

    which = sel[step]
    seen = seen_cont(meta_ref[0], rows, slots)
    for pair in range(q_ref.shape[1] // 128):
        lanes = pl.ds(pair * 128, 128)
        q2, do2 = stacked(q_ref[:, lanes]), stacked(do_ref[:, lanes])
        keys = jnp.concatenate([kp_ref[0, :, lanes], k_ref[:, lanes]], 0)
        values = jnp.concatenate([vp_ref[0, :, lanes], v_ref[:, lanes]], 0)
        probs = probabilities(q2, keys, seen)
        ds = score_grads(probs, do2, values)
        dq = jnp.dot(ds, keys, preferred_element_type=F32)
        dq_ref[:, lanes] = (unstacked(dq) * SCALE).astype(BF)
        dk = dot_tn(ds, q2) * SCALE
        dv = dot_tn(probs.astype(BF), do2)
        dk_ref[:, lanes] = dk[slots:].astype(BF)
        dv_ref[:, lanes] = dv[slots:].astype(BF)
        dkp_ref[which, :, lanes] += dk[:slots]
        dvp_ref[which, :, lanes] += dv[:slots]


def attention_specs(rows, width, slots):
    row = pl.BlockSpec((rows, width), lambda b, sel, *_: (b, 0))
    slot = pl.BlockSpec((1, slots, width), lambda b, sel, *_: (sel[b], 0, 0))
    meta = pl.BlockSpec((1, 1, slots), lambda b, sel, *_: (sel[b], 0, 0))
    rank = pl.BlockSpec((1, rows, 1), lambda b, sel, *_: (b, 0, 0))
    return row, slot, meta, rank


def attend_cont(sel, q, k, v, kp, vp, meta, rows):
    width, slots = q.shape[1], kp.shape[1]
    row, slot, key, _ = attention_specs(rows, width, slots)
    return pl.pallas_call(
        attend_cont_kernel,
        out_shape=jax.ShapeDtypeStruct(q.shape, BF),
        grid_spec=pltpu.PrefetchScalarGridSpec(
            num_scalar_prefetch=1,
            grid=(q.shape[0] // rows,),
            in_specs=[row, row, row, slot, slot, key],
            out_specs=row,
        ),
        name="attend_cont",
    )(sel, q, k, v, kp, vp, meta)


def attend_prompt(sel, q, rank, kp, vp, meta, rows):
    width, slots = q.shape[1], kp.shape[1]
    row, slot, key, ranks = attention_specs(rows, width, slots)
    return pl.pallas_call(
        attend_prompt_kernel,
        out_shape=jax.ShapeDtypeStruct(q.shape, BF),
        grid_spec=pltpu.PrefetchScalarGridSpec(
            num_scalar_prefetch=1,
            grid=(q.shape[0] // rows,),
            in_specs=[row, ranks, slot, slot, key],
            out_specs=row,
        ),
        name="attend_prompt",
    )(sel, q, rank, kp, vp, meta)


def back_prompt(sel, q, do, rank, kp, vp, meta, rows):
    width, slots = q.shape[1], kp.shape[1]
    row, slot, key, ranks = attention_specs(rows, width, slots)
    parts = q.shape[0] // rows
    part = pl.BlockSpec((1, slots, width), lambda b, sel: (b, 0, 0))
    return pl.pallas_call(
        back_prompt_kernel,
        out_shape=(
            jax.ShapeDtypeStruct(q.shape, BF),
            jax.ShapeDtypeStruct((parts, slots, width), F32),
            jax.ShapeDtypeStruct((parts, slots, width), F32),
        ),
        grid_spec=pltpu.PrefetchScalarGridSpec(
            num_scalar_prefetch=1,
            grid=(parts,),
            in_specs=[row, row, ranks, slot, slot, key],
            out_specs=[row, part, part],
        ),
        name="back_prompt",
    )(sel, q, do, rank, kp, vp, meta)


def back_cont(sel, sel_prompt, q, k, v, do, kp, vp, meta, dk_first, dv_first, rows):
    width, slots = q.shape[1], kp.shape[1]
    row, slot, key, _ = attention_specs(rows, width, slots)
    whole = pl.BlockSpec(memory_space=pltpu.VMEM)
    total = jax.ShapeDtypeStruct(kp.shape, F32)
    return pl.pallas_call(
        back_cont_kernel,
        out_shape=(jax.ShapeDtypeStruct(q.shape, BF),) * 3 + (total, total),
        grid_spec=pltpu.PrefetchScalarGridSpec(
            num_scalar_prefetch=2,
            grid=(q.shape[0] // rows,),
            in_specs=[row, row, row, row, slot, slot, key, whole, whole],
            out_specs=[row, row, row, whole, whole],
        ),
        compiler_params=pltpu.CompilerParams(vmem_limit_bytes=56 << 20),
        name="back_cont",
    )(sel, sel_prompt, q, k, v, do, kp, vp, meta, dk_first, dv_first)


def matmul(a, b):
    return jnp.dot(a, b, preferred_element_type=F32)


def matmul_nt(a, b):
    return jnp.einsum("qd,ad->qa", a, b, preferred_element_type=F32)


def matmul_tn(a, b):
    return jnp.einsum("qa,qd->ad", a, b, preferred_element_type=F32)


def scale_of(rows):
    return lax.rsqrt(jnp.mean(rows * rows, -1, keepdims=True) + EPS)


def norm_back(grad, rows, scale, gain):
    moved = gain * grad
    return scale * moved - rows * (scale * scale * scale) * jnp.mean(
        rows * moved, -1, keepdims=True
    )


def gelu_parts(u):
    t = jnp.tanh(ROOT * (u + 0.044715 * u * u * u))
    value = 0.5 * u * (1.0 + t)
    slope = 0.5 * (1.0 + t) + 0.5 * u * (1.0 - t * t) * ROOT * (1.0 + 3.0 * 0.044715 * u * u)
    return value, slope


def slot_table(routes, seq_count, p_dev, pcap):
    prompt_len = p_dev * seq_count // 2
    routed_len = routes.shape[1]
    owners = jnp.arange(seq_count, dtype=jnp.int32)
    owner_prompt = owners // (seq_count // 2)
    owner_base = owners * p_dev - owner_prompt * prompt_len
    owner_routes = routes[owner_prompt]
    below = jnp.sum((owner_routes < owner_base[:, None]).astype(jnp.int32), 1)
    inside = jnp.sum((owner_routes < (owner_base + p_dev)[:, None]).astype(jnp.int32), 1) - below
    slot_ids = jnp.arange(pcap, dtype=jnp.int32)
    slot_rank = below[:, None] + slot_ids[None, :]
    slot_valid = slot_ids[None, :] < inside[:, None]
    picked = jnp.take_along_axis(owner_routes, jnp.clip(slot_rank, 0, routed_len - 1), 1)
    places = jnp.clip(picked - owner_base[:, None], 0, p_dev - 1)
    return slot_rank, slot_valid, places


def pad_rows(rows, count):
    return jnp.pad(rows, ((0, 0), (0, count - rows.shape[1]), (0, 0)))


def part(weights, gains, chunk, slots_x):
    w_query, w_key, w_value, w_out, w_up, w_down = weights
    gain_attn, gain_mlp, router_bf = gains
    router = router_bf.astype(F32)
    n_cont = chunk["xc"].shape[0]
    width = chunk["xc"].shape[1]
    routed = chunk["routed"]
    x_bf = jnp.concatenate([chunk["xc"], chunk["xp"]], 0)
    x = x_bf.astype(F32)
    c1 = scale_of(x)
    n1 = (x * c1 * gain_attn).astype(BF)
    xs = slots_x.reshape(-1, width).astype(F32)
    cs = scale_of(xs)
    ns = (xs * cs * gain_attn).astype(BF)
    n_kv = jnp.concatenate([n1[:n_cont], ns], 0)
    q = matmul(n1, w_query).astype(BF)
    k = matmul(n_kv, w_key).astype(BF)
    v = matmul(n_kv, w_value).astype(BF)
    q_c, q_p = q[:n_cont], q[n_cont:]
    k_c, v_c = k[:n_cont], v[:n_cont]
    meta = chunk["meta"]
    slots = meta.shape[2]
    k_s = k[n_cont:].reshape(-1, slots, width)
    v_s = v[n_cont:].reshape(-1, slots, width)
    sel, sel_prompt, rank = chunk["sel"], chunk["sel_prompt"], chunk["rank"]
    o_c = attend_cont(sel, q_c, k_c, v_c, k_s, v_s, meta, routed)
    o_p = attend_prompt(sel_prompt, q_p, rank, k_s, v_s, meta, PPAD)
    o = jnp.concatenate([o_c, o_p], 0)
    a = matmul(o, w_out)
    h = x + a
    c2 = scale_of(h)
    n2 = (h * c2 * gain_mlp).astype(BF)
    u = matmul(n2, w_up)
    value, slope = gelu_parts(u)
    g = value.astype(BF)
    m = matmul(g, w_down)
    r = 1.0 / (1.0 + jnp.exp(-matmul(x_bf, router_bf[:, None])))
    both = a + m
    y = (x + r * both).astype(BF)

    dy = jnp.concatenate([chunk["dyc"], chunk["dyp"]], 0).astype(F32)
    dz = jnp.sum(dy * both, -1, keepdims=True) * r * (1.0 - r)
    router_grad = jnp.sum(dz * x, 0)
    dx1 = dy + dz * router
    dbranch = dy * r
    dm = dbranch.astype(BF)
    down_grad = matmul_tn(g, dm)
    du = (matmul_nt(dm, w_down) * slope).astype(BF)
    up_grad = matmul_tn(n2, du)
    dn2 = matmul_nt(du, w_up)
    dh = norm_back(dn2, h, c2, gain_mlp)
    gain_mlp_grad = jnp.sum(dn2 * h * c2, 0)
    da = (dbranch + dh).astype(BF)
    out_grad = matmul_tn(o, da)
    do = matmul_nt(da, w_out).astype(BF)
    dq_p, dk_first, dv_first = back_prompt(
        sel_prompt, q_p, do[n_cont:], rank, k_s, v_s, meta, PPAD
    )
    dq_c, dk_c, dv_c, dk_s, dv_s = back_cont(
        sel, sel_prompt, q_c, k_c, v_c, do[:n_cont], k_s, v_s, meta, dk_first, dv_first, routed
    )
    dq = jnp.concatenate([dq_c, dq_p], 0)
    dk = jnp.concatenate([dk_c, dk_s.reshape(-1, width).astype(BF)], 0)
    dv = jnp.concatenate([dv_c, dv_s.reshape(-1, width).astype(BF)], 0)
    query_grad = matmul_tn(n1, dq)
    key_grad = matmul_tn(n_kv, dk)
    value_grad = matmul_tn(n_kv, dv)
    dn_q = matmul_nt(dq, w_query)
    dn_kv = matmul_nt(dk, w_key) + matmul_nt(dv, w_value)
    dn_c = dn_q[:n_cont] + dn_kv[:n_cont]
    dn_p, dn_s = dn_q[n_cont:], dn_kv[n_cont:]
    gain_attn_grad = (
        jnp.sum(dn_c * x[:n_cont] * c1[:n_cont], 0)
        + jnp.sum(dn_p * x[n_cont:] * c1[n_cont:], 0)
        + jnp.sum(dn_s * xs * cs, 0)
    )
    dx_rest = dx1 + dh
    dx_c = (
        dx_rest[:n_cont] + norm_back(dn_c, x[:n_cont], c1[:n_cont], gain_attn)
    ).astype(BF)
    grads = (query_grad, key_grad, value_grad, out_grad, up_grad, down_grad)
    small = (gain_attn_grad, gain_mlp_grad, router_grad)
    tail = (dn_p, dx_rest[n_cont:], x[n_cont:], c1[n_cont:])
    return y, dx_c, grads, small, dn_s, tail


def finish_prompt(tail, received, gain_attn, pcap):
    dn_p, rest, x, c1 = tail
    width = x.shape[1]
    count = received.shape[0]
    dn = dn_p + pad_rows(received, PPAD).reshape(-1, width)
    dx = (rest + norm_back(dn, x, c1, gain_attn)).astype(BF)
    return dx.reshape(count, PPAD, width)


def body(
    prompt_x,
    cont_x,
    prompt_routes,
    cont_routes,
    cont_group,
    w_query,
    w_key,
    w_value,
    w_out,
    w_up,
    w_down,
    gain_attn,
    gain_mlp,
    w_router,
    prompt_cot,
    cont_cot,
):
    seq_count = lax.axis_size("seq")
    grp_count = lax.axis_size("grp")
    tuned = seq_count == 16 and grp_count == 2
    seq_index = lax.axis_index("seq")
    micro, p_dev, width = prompt_x.shape[0], prompt_x.shape[2], prompt_x.shape[3]
    conts, length, routed = cont_x.shape[2], cont_x.shape[3], cont_routes.shape[3]
    pcap = 3 * p_dev // 16
    own_prompt = seq_index // (seq_count // 2)
    group = 2 if micro % 2 == 0 else 1
    shards = (w_query, w_key, w_value, w_out, w_up, w_down)

    tables = [slot_table(prompt_routes[m, 0], seq_count, p_dev, pcap) for m in range(micro)]
    metas, ranks, places, rows_p, dys_p = [], [], [], [], []
    for m in range(micro):
        slot_rank, slot_valid, slot_places = tables[m]
        metas.append(jnp.where(slot_valid, slot_rank, FAR).reshape(2, 1, -1))
        pick = lambda t: lax.dynamic_index_in_dim(t, seq_index, 0, keepdims=False)
        valid, rank, place = pick(slot_valid), pick(slot_rank), pick(slot_places)
        ranks.append(jnp.pad(jnp.where(valid, rank, -1), (0, PPAD - pcap), constant_values=-1))
        places.append(jnp.pad(jnp.where(valid, place, -1), (0, PPAD - pcap), constant_values=-1))
        rows_p.append(jnp.take(prompt_x[m, 0], place, axis=0))
        dy = jnp.take(prompt_cot[m, 0], place, axis=0)
        dys_p.append(jnp.where(valid[:, None], dy, jnp.zeros_like(dy)))
    places = jnp.stack(places)
    xc = jnp.take_along_axis(cont_x[:, 0], cont_routes[:, 0, :, :, None], 2)
    dyc = jnp.take_along_axis(cont_cot[:, 0], cont_routes[:, 0, :, :, None], 2)

    if tuned:
        tiny = jnp.pad(
            jnp.concatenate([gain_attn, gain_mlp, w_router])[None, :], ((0, 7), (0, 32))
        )
        up4 = w_up.reshape(4, 8, -1)
        down4 = w_down.reshape(4, -1, width)
        arrays = rows_p + [tiny, w_query, w_key, w_value, w_out]
        routes = "ab" * (micro // 2) + "a" * (micro % 2) + "ABABA"
        arrays += [w_up, w_down]
        routes += "BA"
        got = gather_call(arrays, routes, 5)
        slots_x = jnp.stack(got[:micro])
        tiny = got[micro].reshape(32, 8, 128)
        vectors = tuple(tiny[:, 0, 32 * i : 32 * i + 32].reshape(-1) for i in range(3))
        weights = tuple(t.reshape(-1, t.shape[-1]) for t in got[micro + 1 :])
    else:
        gather = lambda t: lax.all_gather(t, ("grp", "seq"), axis=0, tiled=True)
        slots_x = lax.all_gather(jnp.stack(rows_p), "seq", axis=1, tiled=False)
        weights = tuple(gather(t) for t in shards)
        vectors = tuple(gather(t) for t in (gain_attn, gain_mlp, w_router))
    gains = (vectors[0].astype(F32), vectors[1].astype(F32), vectors[2])
    slots_x = slots_x.reshape(micro, 2, -1, width)

    totals = None
    ys, dxs, slot_grads, tails = [], [], [], []
    for start in range(0, micro, group):
        mine = slice(start, start + group)
        sel = (
            jnp.arange(group, dtype=jnp.int32)[:, None] * 2 + cont_group[mine, 0]
        ).reshape(-1)
        chunk = dict(
            routed=routed,
            xc=xc[mine].reshape(-1, width),
            xp=pad_rows(jnp.stack(rows_p[mine]), PPAD).reshape(-1, width),
            dyc=dyc[mine].reshape(-1, width),
            dyp=pad_rows(jnp.stack(dys_p[mine]), PPAD).reshape(-1, width),
            meta=jnp.concatenate(metas[mine], 0),
            rank=jnp.stack(ranks[mine])[:, :, None],
            sel=sel,
            sel_prompt=jnp.arange(group, dtype=jnp.int32) * 2 + own_prompt,
        )
        y, dx_c, grads, small, dn_s, tail = part(weights, gains, chunk, slots_x[mine])
        ys.append(y)
        dxs.append(dx_c)
        slot_grads.append(dn_s.astype(BF).reshape(group, seq_count, pcap, width))
        tails.append(tail)
        new = tuple(grads) + tuple(small)
        totals = new if totals is None else tuple(a + b for a, b in zip(totals, new))

    if tuned:
        split = lambda t: t.astype(BF).reshape((2,) + ZYX + (-1, t.shape[-1]))
        small = jnp.concatenate([t.reshape(32, 1, 32) for t in totals[6:]], 2)
        small = jnp.pad(small, ((0, 0), (0, 7), (0, 32))).reshape((2,) + ZYX + (8, 128))
        slot_list = [slot_grads[m // group][m % group] for m in range(micro)]
        arrays = [split(t) for t in totals[:6]] + [small]
        arrays += [t.reshape(ZYX + (pcap, width)) for t in slot_list]
        shapes = [t.shape for t in shards] + [(8, 128)] + [(pcap, width)] * micro
        out = scatter_call(arrays, shapes, micro, 32)
        final = tuple(out[:6]) + tuple(out[6][0, 32 * i : 32 * i + 32] for i in range(3))
        received = jnp.stack(out[7:])
    else:
        final = tuple(
            lax.psum_scatter(t, ("grp", "seq"), scatter_dimension=0, tiled=True) for t in totals
        )
        received = lax.psum_scatter(
            jnp.concatenate(slot_grads, 0), "seq", scatter_dimension=1, tiled=False
        ).astype(F32)

    y_c = jnp.concatenate([t[: group * conts * routed] for t in ys], 0)
    y_p = jnp.concatenate([t[group * conts * routed :] for t in ys], 0)
    dx_c = jnp.concatenate(dxs, 0)
    dx_p = jnp.concatenate(
        [
            finish_prompt(tail, received[i * group : (i + 1) * group], gains[0], pcap)
            for i, tail in enumerate(tails)
        ],
        0,
    )
    flat = lambda t: t.reshape((-1,) + t.shape[-2:])
    rows_of = lambda t: t.reshape(-1, routed, width)
    idx_c = cont_routes.reshape(-1, routed)
    prompt_out = place_rows(flat(prompt_x), places, y_p.reshape(-1, PPAD, width))
    cont_out = place_rows(flat(cont_x), idx_c, rows_of(y_c))
    cont_grad = place_rows(flat(cont_cot), idx_c, rows_of(dx_c))
    prompt_grad = place_rows(flat(prompt_cot), places, dx_p)
    return (
        prompt_out.reshape(prompt_x.shape),
        cont_out.reshape(cont_x.shape),
        prompt_grad.reshape(prompt_x.shape),
        cont_grad.reshape(cont_x.shape),
    ) + final


def solution(mesh):
    both = ("grp", "seq")
    in_specs = (
        P(None, "grp", "seq", None),
        P(None, "grp", "seq", None, None),
        P(None, "grp", None, None),
        P(None, "grp", "seq", None),
        P(None, "grp", "seq"),
    )
    in_specs += (P(both, None),) * 6 + (P(both),) * 3
    in_specs += (P(None, "grp", "seq", None), P(None, "grp", "seq", None, None))
    out_specs = (
        P(None, "grp", "seq", None),
        P(None, "grp", "seq", None, None),
        P(None, "grp", "seq", None),
        P(None, "grp", "seq", None, None),
    )
    out_specs += (P(both, None),) * 6 + (P(both),) * 3
    return jax.shard_map(body, mesh=mesh, in_specs=in_specs, out_specs=out_specs, check_vma=False)
```
